32 devices in a mesh: member: 4 (over x, core), space: 8 (over z, y).
Axes of the slice: x: 2, y: 2, z: 4, core: 2. Of those that a mesh axis runs over, the one named last changes fastest.
Arguments:
- features: bfloat16 [4, 641, 192, 128], P('member', None, 'space'), may hold values from -6 to 6
- depth_kernel: float32 [641, 5, 5], replicated, may hold values from -1.25 to 1.25
- in_weight: bfloat16 [641, 1282], replicated, may hold values from -0.25 to 0.25
- out_weight: bfloat16 [1282, 641], replicated, may hold values from -0.15625 to 0.15625
- decoder_weight: bfloat16 [641, 72], replicated, may hold values from -0.25 to 0.25
- observed: float32 [72, 192, 128], P(None, 'space'), may hold values from -6 to 6
- land_mask: int32 [192, 128], P('space'), may hold values 0 or 1
Outputs:
- grad_features: bfloat16 [4, 641, 192, 128], P('member', None, 'space')
- decoder_grad: float32 [641, 72], replicated
The draws below stay inside these ranges and needn't reach their ends.
All inputs are finite; a program needn't handle non-finite values. No bound on the sum of `land_mask` on one device may be relied on, other than what follows from the above.
Results may differ from the reference program's by a relative error of at most 0.0054.
Values may be sent and summed in bfloat16 or wider, within the bound.
A program may use at most 128 MiB of HBM per device.

```python
import math
import jax
import jax.numpy as jnp
from jax import lax

C = 641
HID = 1282
OUT = 72
LAT = 128
MEMBERS = 4
LON = 192


def with_ends(drawn, stream_key, least, largest):
    dims = drawn.shape
    index_at = [jax.random.randint(jax.random.fold_in(stream_key, axis), (), 0, dims[axis]) for axis in range(len(dims))]
    drawn = drawn.at[tuple(index_at)].set(least)
    longest = dims.index(max(dims))
    index_at[longest] = (index_at[longest] + 1) % dims[longest]
    return drawn.at[tuple(index_at)].set(largest)


def steps_of(rng, dims, pieces, smallest, high):
    gain = 1.0
    for dim, blocks in pieces:
        heights = jax.random.uniform(jax.random.fold_in(jax.random.fold_in(rng, 6), dim), (blocks,), jnp.float32, smallest / len(pieces), high / len(pieces))
        gain = gain * jnp.repeat(jnp.exp(heights), dims[dim] // blocks).reshape((-1,) + (1,) * (len(dims) - 1 - dim))
    return gain


def noise(rng, extent, deviation, reach, cuts=(), dtype=jnp.bfloat16):
    drawn = jax.random.normal(rng, extent, jnp.float32) * deviation
    if len(cuts) > 0:
        drawn = steps_of(rng, extent, cuts, -0.22, 0.18) * drawn
    return jnp.clip(drawn, min=-reach, max=reach).astype(dtype)


def setup_inputs(seed: int = 0) -> dict:
    streams_of = jax.random.split(jax.random.key(seed), 8)
    return {
        "features": noise(streams_of[0], (MEMBERS, C, LON, LAT), 1.0, 6.0, ((0, 4), (2, 8))),
        "depth_kernel": noise(streams_of[1], (C, 5, 5), 25 ** -0.5, 1.25, (), jnp.float32),
        "in_weight": noise(streams_of[2], (C, HID), C ** -0.5, 0.25),
        "out_weight": noise(streams_of[3], (HID, C), HID ** -0.5, 0.15625),
        "decoder_weight": noise(streams_of[4], (C, OUT), C ** -0.5, 0.25),
        "observed": noise(streams_of[5], (OUT, LON, LAT), 1.0, 6.0, ((1, 8),), jnp.float32),
        "land_mask": with_ends((jax.random.randint(streams_of[6], (LON, LAT), 0, 10) < 3).astype(jnp.int32), jax.random.fold_in(streams_of[6], 1), 0, 1),
    }


norm_eps = 1e-05

def convolve(field, depth_kernel):
    lat_len = field.shape[2]
    widened = jnp.pad(field.astype(jnp.float32), ((0, 0), (0, 0), (2, 2)))
    total = jnp.zeros(field.shape, jnp.float32)
    for row_off in range(5):
        rolled = jnp.roll(widened, 2 - row_off, axis=1)
        for col_off in range(5):
            total = total + depth_kernel[:, row_off, col_off][:, None, None] * rolled[:, :, col_off:col_off + lat_len]
    return total

def forward(field, depth_kernel, in_weight, out_weight, decoder_weight):
    channels = field.shape[0]
    convolved = convolve(field, depth_kernel)
    center = lax.optimization_barrier(jnp.mean(convolved, axis=0, keepdims=True))
    shifted = convolved - center
    normed = (shifted * lax.rsqrt(lax.optimization_barrier(jnp.mean(shifted * shifted, axis=0, keepdims=True)) + norm_eps)).astype(jnp.bfloat16)
    flat = normed.reshape(channels, -1)
    hidden = jax.nn.gelu(jnp.dot(in_weight.T, flat, preferred_element_type=jnp.float32), approximate=False).astype(jnp.bfloat16)
    mlp_out = jnp.dot(out_weight.T, hidden, preferred_element_type=jnp.float32)
    block_out = (field.reshape(channels, -1).astype(jnp.float32) + mlp_out).astype(jnp.bfloat16)
    decoded = jnp.dot(decoder_weight.T, block_out, preferred_element_type=jnp.float32).astype(jnp.bfloat16)
    return (block_out, decoded)

def reference(features, depth_kernel, in_weight, out_weight, decoder_weight, observed, land_mask):
    members = features.shape[0]
    channels = features.shape[1]
    points = features.shape[2] * features.shape[3]
    block_out, decoded = lax.map(lambda field: forward(field, depth_kernel, in_weight, out_weight, decoder_weight), features)
    decoded_f = decoded.astype(jnp.float32)
    obs_flat = observed.reshape(observed.shape[0], -1)
    point_weight = (4.0 + 8.0 * land_mask.astype(jnp.float32)).reshape(-1)
    misfit = decoded_f - obs_flat[None]
    misfit_norm = jnp.sqrt(lax.optimization_barrier(jnp.sum(misfit * misfit, axis=1, keepdims=True)) + 1.0)

    def add_pair(other, total):
        apart = decoded_f - lax.dynamic_index_in_dim(decoded_f, other, 0, True)
        return total + apart / jnp.sqrt(lax.optimization_barrier(jnp.sum(apart * apart, axis=1, keepdims=True)) + 1.0)
    pair_sum = lax.fori_loop(0, members, add_pair, jnp.zeros(decoded_f.shape, jnp.float32))
    score_grad = (point_weight[None, None, :] * (misfit / misfit_norm - pair_sum / members)).astype(jnp.bfloat16)
    grad_flat = lax.map(lambda grad_one: jnp.dot(decoder_weight, grad_one, preferred_element_type=jnp.float32).astype(jnp.bfloat16), score_grad)
    grad_features = grad_flat.reshape(features.shape)

    def add_term(total, pair):
        return (total + jnp.dot(pair[0], pair[1].T, preferred_element_type=jnp.float32), None)
    summed, _ = lax.scan(add_term, jnp.zeros((channels, decoder_weight.shape[1]), jnp.float32), (block_out, score_grad))
    decoder_grad = summed / math.sqrt(members * points)
    return (grad_features, decoder_grad)
```

```python
import functools
import math

import jax
import jax.numpy as jnp
from jax import lax
from jax.experimental import pallas as pl
from jax.experimental.pallas import tpu as pltpu
from jax.sharding import PartitionSpec as P

norm_eps = 1e-05
MESH = pl.DeviceIdType.MESH
VMEM_SPEC = pl.BlockSpec(memory_space=pltpu.VMEM)


def round_up(value, step):
    return -(-value // step) * step


def gelu(x):
    return 0.5 * x * (1.0 + lax.erf(x * (0.5**0.5)))


def forward_kernel(
    channels, rows_at_once, x_ref, left_ref, right_ref, taps_ref, w1_ref, w2_ref, dec_ref,
    block_ref, decoded_ref, conv_ref, sum_ref, wide_ref,
):
    lon_len, padded_c, lat_len = x_ref.shape
    half = left_ref.shape[0]
    size = 2 * half + 1
    blocks = padded_c // 16
    lane = lax.broadcasted_iota(jnp.int32, (16, lat_len), 1)
    sum_ref[...] = jnp.zeros_like(sum_ref)

    def conv_block(block, carry):
        chan = pl.ds(pl.multiple_of(block * 16, 16), 16)
        for i in range(half):
            wide_ref[i] = left_ref[i, chan, :].astype(jnp.float32)
            wide_ref[half + lon_len + i] = right_ref[i, chan, :].astype(jnp.float32)
        for i in range(lon_len):
            wide_ref[half + i] = x_ref[i, chan, :].astype(jnp.float32)
        total = [None] * lon_len
        for q in range(size):
            coef = [
                jnp.broadcast_to(taps_ref[chan, p * size + q : p * size + q + 1], (16, lat_len))
                for p in range(size)
            ]
            shift = half - q
            for i in range(lon_len):
                part = coef[0] * wide_ref[i]
                for p in range(1, size):
                    part = part + coef[p] * wide_ref[i + p]
                if shift != 0:
                    part = pltpu.roll(part, shift % lat_len, 1)
                    inside = lane >= shift if shift > 0 else lane < lat_len + shift
                    part = jnp.where(inside, part, 0.0)
                if q == 0:
                    conv_ref[i, chan, :] = part
                else:
                    part = part + conv_ref[i, chan, :]
                    conv_ref[i, chan, :] = part
                if q == size - 1:
                    sum_ref[i] = sum_ref[i] + part[0:8] + part[8:16]
        return carry

    lax.fori_loop(0, blocks, conv_block, 0)

    last = padded_c - 16
    row_at = lax.broadcasted_iota(jnp.int32, (16, lat_len), 0)
    real = row_at < channels - last

    def rows_step(step, carry):
        normed_rows = []
        for r in range(rows_at_once):
            row = step * rows_at_once + r
            center = jnp.sum(sum_ref[row], axis=0, keepdims=True) * (1.0 / channels)
            head = conv_ref[row, 0:last, :] - center
            tail = jnp.where(real, conv_ref[row, last:padded_c, :] - center, 0.0)
            square = jnp.sum(head * head, axis=0, keepdims=True) + jnp.sum(
                tail * tail, axis=0, keepdims=True
            )
            scale = lax.rsqrt(square * (1.0 / channels) + norm_eps)
            normed_rows.append(
                jnp.concatenate(
                    [(head * scale).astype(jnp.bfloat16), (tail * scale).astype(jnp.bfloat16)],
                    axis=0,
                )
            )
        normed = jnp.concatenate(normed_rows, axis=1)
        hid = w1_ref.shape[0]
        piece = hid // 3
        out = None
        for k in range(3):
            pre = jnp.dot(
                w1_ref[k * piece : (k + 1) * piece, :], normed, preferred_element_type=jnp.float32
            )
            act = gelu(pre).astype(jnp.bfloat16)
            part = jnp.dot(w2_ref[k], act, preferred_element_type=jnp.float32)
            out = part if out is None else out + part
        feats = jnp.concatenate(
            [x_ref[step * rows_at_once + r] for r in range(rows_at_once)], axis=1
        ).astype(jnp.float32)
        block_out = (feats + out).astype(jnp.bfloat16)
        decoded = jnp.dot(dec_ref[...], block_out, preferred_element_type=jnp.float32).astype(
            jnp.bfloat16
        )
        for r in range(rows_at_once):
            cols = slice(r * lat_len, (r + 1) * lat_len)
            block_ref[step * rows_at_once + r] = block_out[:, cols]
            decoded_ref[step * rows_at_once + r] = decoded[:, cols]
        return carry

    lax.fori_loop(0, lon_len // rows_at_once, rows_step, 0)


def score_kernel(
    rows_at_once, scale, every_ref, own_ref, block_ref, observed_ref, weight_ref, dec_ref,
    grad_ref, term_ref,
):
    members = every_ref.shape[0]
    lon_len, outputs, lat_len = own_ref.shape
    term_ref[...] = jnp.zeros_like(term_ref)

    def rows_step(step, carry):
        score_rows = []
        for r in range(rows_at_once):
            row = step * rows_at_once + r
            own = own_ref[row].astype(jnp.float32)
            misfit = own - observed_ref[row]
            total = misfit * lax.rsqrt(jnp.sum(misfit * misfit, axis=0, keepdims=True) + 1.0)
            pair_sum = jnp.zeros_like(own)
            for k in range(members):
                apart = own - every_ref[k, row].astype(jnp.float32)
                pair_sum = pair_sum + apart * lax.rsqrt(
                    jnp.sum(apart * apart, axis=0, keepdims=True) + 1.0
                )
            weight = weight_ref[pl.ds(row, 1), :]
            score_rows.append((weight * (total - pair_sum / members)).astype(jnp.bfloat16))
        score = jnp.concatenate(score_rows, axis=1)
        block = jnp.concatenate(
            [block_ref[step * rows_at_once + r] for r in range(rows_at_once)], axis=1
        )
        grad = jnp.dot(dec_ref[...], score, preferred_element_type=jnp.float32).astype(jnp.bfloat16)
        for r in range(rows_at_once):
            grad_ref[step * rows_at_once + r] = grad[:, r * lat_len : (r + 1) * lat_len]
        term_ref[...] += scale * lax.dot_general(
            score, block, (((1,), (1,)), ((), ())), preferred_element_type=jnp.float32
        )
        return carry

    lax.fori_loop(0, lon_len // rows_at_once, rows_step, 0)


def reduce_kernel(groups, term_ref, out_ref, mine, got, own, whole, sems):
    send1, recv1, send2, recv2 = (sems.at[i] for i in range(4))
    member_n, space_n = groups
    n = member_n * space_n
    per = own.shape[0]
    me = lax.axis_index("member") * space_n + lax.axis_index("space")

    def peer(e):
        other = lax.rem(me + e + 1, n)
        return other, (other // space_n, lax.rem(other, space_n))

    barrier = pltpu.get_barrier_semaphore()

    def greet(e, carry):
        pl.semaphore_signal(barrier, inc=1, device_id=peer(e)[1], device_id_type=MESH)
        return carry

    lax.fori_loop(0, n - 1, greet, 0)
    tall = term_ref.shape[0] // 8
    across = term_ref.shape[1] // 128
    for a in range(tall):
        for b in range(across):
            at = a * across + b
            mine[at // per, at % per] = term_ref[8 * a : 8 * a + 8, 128 * b : 128 * b + 128]
    for at in range(tall * across, n * per):
        mine[at // per, at % per] = jnp.zeros((8, 128), jnp.float32)
    pl.semaphore_wait(barrier, n - 1)

    def scatter_copy(e):
        other, device = peer(e)
        return pltpu.make_async_remote_copy(
            src_ref=mine.at[other], dst_ref=got.at[e], send_sem=send1.at[e], recv_sem=recv1.at[e],
            device_id=device, device_id_type=MESH,
        )

    def gather_copy(e):
        _, device = peer(e)
        return pltpu.make_async_remote_copy(
            src_ref=own, dst_ref=whole.at[e], send_sem=send2.at[e], recv_sem=recv2.at[e],
            device_id=device, device_id_type=MESH,
        )

    def start(make):
        def body(e, carry):
            make(e).start()
            return carry

        lax.fori_loop(0, n - 1, body, 0)

    def finish(make):
        def body(e, carry):
            make(e).wait()
            return carry

        lax.fori_loop(0, n - 1, body, 0)

    start(scatter_copy)
    finish(scatter_copy)
    total = mine[me]
    for e in range(n - 1):
        total = total + got[e]
    own[...] = total
    start(gather_copy)
    out_ref[me] = total
    finish(gather_copy)
    for e in range(n - 1):
        out_ref[lax.rem(me + n - e - 1, n)] = whole[e]


def per_device(features, depth_kernel, in_weight, out_weight, decoder_weight, observed, land_mask):
    _, channels, lon_len, lat_len = features.shape
    hid = in_weight.shape[1]
    outputs = decoder_weight.shape[1]
    size = depth_kernel.shape[1]
    half = size // 2
    member_n = lax.axis_size("member")
    space_n = lax.axis_size("space")
    n = member_n * space_n
    members = features.shape[0] * member_n
    total_points = lon_len * space_n * lat_len
    padded_c = round_up(channels, 16)
    padded_h = round_up(hid, 48)
    more_c = padded_c - channels
    more_h = padded_h - hid

    x = jnp.pad(jnp.transpose(features[0], (1, 0, 2)), ((0, 0), (0, more_c), (0, 0)))
    forth = [(i, (i + 1) % space_n) for i in range(space_n)]
    back = [((i + 1) % space_n, i) for i in range(space_n)]
    left = lax.ppermute(x[lon_len - half :], "space", forth)
    right = lax.ppermute(x[:half], "space", back)
    taps = jnp.pad(depth_kernel.reshape(channels, size * size), ((0, more_c), (0, 0)))
    w1 = jnp.pad(in_weight.T, ((0, more_h), (0, more_c)))
    w2 = jnp.pad(out_weight.T, ((0, more_c), (0, more_h)))
    w2 = jnp.stack(jnp.split(w2, 3, axis=1))
    dec_t = jnp.pad(decoder_weight.T, ((0, 0), (0, more_c)))
    block_out, decoded = pl.pallas_call(
        functools.partial(forward_kernel, channels, 2),
        name="forward",
        out_shape=(
            jax.ShapeDtypeStruct((lon_len, padded_c, lat_len), jnp.bfloat16),
            jax.ShapeDtypeStruct((lon_len, outputs, lat_len), jnp.bfloat16),
        ),
        in_specs=[VMEM_SPEC] * 7,
        out_specs=[VMEM_SPEC] * 2,
        scratch_shapes=[
            pltpu.VMEM((lon_len, padded_c, lat_len), jnp.float32),
            pltpu.VMEM((lon_len, 8, lat_len), jnp.float32),
            pltpu.VMEM((lon_len + 2 * half, 16, lat_len), jnp.float32),
        ],
    )(x, left, right, taps, w1, w2, dec_t)
    every = lax.all_gather(decoded, "member", axis=0)
    weight = 4.0 + 8.0 * land_mask.astype(jnp.float32)
    grad, term = pl.pallas_call(
        functools.partial(score_kernel, 2, 1.0 / math.sqrt(members * total_points)),
        name="score",
        out_shape=(
            jax.ShapeDtypeStruct((lon_len, channels, lat_len), jnp.bfloat16),
            jax.ShapeDtypeStruct((outputs, padded_c), jnp.float32),
        ),
        in_specs=[VMEM_SPEC] * 6,
        out_specs=[VMEM_SPEC] * 2,
    )(every, decoded, block_out, jnp.transpose(observed, (1, 0, 2)), weight, decoder_weight)
    wide_c = round_up(padded_c, 128)
    tiles = (outputs // 8) * (wide_c // 128)
    per = -(-tiles // n)
    summed = pl.pallas_call(
        functools.partial(reduce_kernel, (member_n, space_n)),
        name="reduce",
        out_shape=jax.ShapeDtypeStruct((n, per, 8, 128), jnp.float32),
        in_specs=[VMEM_SPEC],
        out_specs=VMEM_SPEC,
        scratch_shapes=[
            pltpu.VMEM((n, per, 8, 128), jnp.float32),
            pltpu.VMEM((n - 1, per, 8, 128), jnp.float32),
            pltpu.VMEM((per, 8, 128), jnp.float32),
            pltpu.VMEM((n - 1, per, 8, 128), jnp.float32),
            pltpu.SemaphoreType.DMA((4, n - 1)),
        ],
        compiler_params=pltpu.CompilerParams(collective_id=0, has_side_effects=True),
    )(jnp.pad(term, ((0, 0), (0, wide_c - padded_c))))
    flat = summed.reshape(n * per, 8, 128)[:tiles].reshape(outputs // 8, wide_c // 128, 8, 128)
    decoder_grad = jnp.transpose(flat, (0, 2, 1, 3)).reshape(outputs, wide_c)[:, :channels].T
    grad_features = jnp.transpose(grad, (1, 0, 2))[None]
    return (grad_features, decoder_grad)


def solution(mesh):
    placed = (
        P("member", None, "space", None),
        P(),
        P(),
        P(),
        P(),
        P(None, "space", None),
        P("space", None),
    )
    return jax.shard_map(
        per_device,
        mesh=mesh,
        in_specs=placed,
        out_specs=(P("member", None, "space", None), P()),
        check_vma=False,
    )
```

```python
import functools
import math

import jax
import jax.numpy as jnp
from jax import lax
from jax.experimental import pallas as pl
from jax.experimental.pallas import tpu as pltpu
from jax.sharding import PartitionSpec as P

norm_eps = 1e-05
MESH = pl.DeviceIdType.MESH
VMEM_SPEC = pl.BlockSpec(memory_space=pltpu.VMEM)


def round_up(value, step):
    return -(-value // step) * step


def gelu(x):
    return 0.5 * x * (1.0 + lax.erf(x * (0.5**0.5)))


def conv_kernel(x_ref, left_ref, right_ref, taps_ref, normed_ref, conv_ref, sum_ref, wide_ref):
    lon_len, channels, lat_len = x_ref.shape
    half = left_ref.shape[0]
    size = 2 * half + 1
    full = channels // 16
    rest = channels - full * 16
    lane = lax.broadcasted_iota(jnp.int32, (16, lat_len), 1)
    sum_ref[...] = jnp.zeros_like(sum_ref)

    def convolve(chan):
        for q in range(size):
            coef = [
                jnp.broadcast_to(taps_ref[chan, p * size + q : p * size + q + 1], (16, lat_len))
                for p in range(size)
            ]
            shift = half - q
            for i in range(lon_len):
                part = coef[0] * wide_ref[i]
                for p in range(1, size):
                    part = part + coef[p] * wide_ref[i + p]
                if shift != 0:
                    part = pltpu.roll(part, shift % lat_len, 1)
                    inside = lane >= shift if shift > 0 else lane < lat_len + shift
                    part = jnp.where(inside, part, 0.0)
                if q > 0:
                    part = part + conv_ref[i, chan, :]
                conv_ref[i, chan, :] = part
                if q == size - 1:
                    sum_ref[i] = sum_ref[i] + part[0:8] + part[8:16]

    def conv_block(block, carry):
        chan = pl.ds(pl.multiple_of(block * 16, 16), 16)
        for i in range(half):
            wide_ref[i] = left_ref[i, chan, :].astype(jnp.float32)
            wide_ref[half + lon_len + i] = right_ref[i, chan, :].astype(jnp.float32)
        for i in range(lon_len):
            wide_ref[half + i] = x_ref[i, chan, :].astype(jnp.float32)
        convolve(chan)
        return carry

    lax.fori_loop(0, full, conv_block, 0)
    if rest > 0:
        wide_ref[...] = jnp.zeros_like(wide_ref)
        for i in range(half):
            wide_ref[i, 0:rest, :] = left_ref[i, full * 16 : channels, :].astype(jnp.float32)
            wide_ref[half + lon_len + i, 0:rest, :] = right_ref[i, full * 16 : channels, :].astype(
                jnp.float32
            )
        for i in range(lon_len):
            wide_ref[half + i, 0:rest, :] = x_ref[i, full * 16 : channels, :].astype(jnp.float32)
        convolve(slice(full * 16, full * 16 + 16))

    def norm_row(row, carry):
        center = jnp.sum(sum_ref[row], axis=0, keepdims=True) * (1.0 / channels)
        shifted = conv_ref[row, 0:channels, :] - center
        square = jnp.sum(shifted * shifted, axis=0, keepdims=True)
        scale = lax.rsqrt(square * (1.0 / channels) + norm_eps)
        normed_ref[row] = (shifted * scale).astype(jnp.bfloat16)
        return carry

    lax.fori_loop(0, lon_len, norm_row, 0)


def cuts_of(hid):
    width = round_up(-(-hid // 3), 256)
    return [(at, min(at + width, hid)) for at in range(0, hid, width)]


def main_kernel(
    groups, rows_at_once, scale, x_ref, normed_ref, w1_ref, w2_ref, dect_ref, dec_ref, observed_ref,
    weight_ref, grad_ref, out_ref, block_ref, own_ref, others_ref, score_ref, term_ref, mine, got,
    mine_sum, whole, pair_sems, sems,
):
    lon_len, channels, lat_len = x_ref.shape
    member_n, space_n = groups
    n = member_n * space_n
    member = lax.axis_index("member")
    space = lax.axis_index("space")
    me = member * space_n + space
    steps = lon_len // rows_at_once

    def peer(e):
        other = lax.rem(me + e + 1, n)
        return other, (other // space_n, lax.rem(other, space_n))

    barrier = pltpu.get_barrier_semaphore()

    def greet(e, carry):
        pl.semaphore_signal(barrier, inc=1, device_id=peer(e)[1], device_id_type=MESH)
        return carry

    lax.fori_loop(0, n - 1, greet, 0)

    def joined(ref, step):
        return jnp.concatenate([ref[step * rows_at_once + r] for r in range(rows_at_once)], axis=1)

    def mlp_step(step):
        normed = joined(normed_ref, step)
        out = joined(x_ref, step).astype(jnp.float32)
        for low, high in cuts_of(w1_ref.shape[0]):
            pre = jnp.dot(w1_ref[low:high, :], normed, preferred_element_type=jnp.float32)
            act = gelu(pre).astype(jnp.bfloat16)
            out = out + jnp.dot(w2_ref[:, low:high], act, preferred_element_type=jnp.float32)
        block_out = out.astype(jnp.bfloat16)
        decoded = jnp.dot(dect_ref[...], block_out, preferred_element_type=jnp.float32).astype(
            jnp.bfloat16
        )
        for r in range(rows_at_once):
            cols = slice(r * lat_len, (r + 1) * lat_len)
            block_ref[step * rows_at_once + r] = block_out[:, cols]
            own_ref[step * rows_at_once + r] = decoded[:, cols]

    def pair_copy(step, j):
        rows = pl.ds(step * rows_at_once, rows_at_once)
        return pltpu.make_async_remote_copy(
            src_ref=own_ref.at[rows], dst_ref=others_ref.at[j, rows],
            send_sem=pair_sems.at[0, j, step], recv_sem=pair_sems.at[1, j, step],
            device_id=(lax.rem(member + j + 1, member_n), space), device_id_type=MESH,
        )

    mlp_step(0)
    pl.semaphore_wait(barrier, n - 1)
    for j in range(member_n - 1):
        pair_copy(0, j).start()

    def mlp_loop(step, carry):
        mlp_step(step)
        for j in range(member_n - 1):
            pair_copy(step, j).start()
        return carry

    lax.fori_loop(1, steps, mlp_loop, 0)
    term_ref[...] = jnp.zeros_like(term_ref)

    def score_step(step, carry):
        for j in range(member_n - 1):
            pair_copy(step, j).wait()
        for r in range(rows_at_once):
            row = step * rows_at_once + r
            own = own_ref[row].astype(jnp.float32)
            misfit = own - observed_ref[row]
            total = misfit * lax.rsqrt(jnp.sum(misfit * misfit, axis=0, keepdims=True) + 1.0)
            pair_sum = jnp.zeros_like(own)
            for k in range(member_n):
                other = own_ref[row] if k == member_n - 1 else others_ref[k, row]
                apart = own - other.astype(jnp.float32)
                pair_sum = pair_sum + apart * lax.rsqrt(
                    jnp.sum(apart * apart, axis=0, keepdims=True) + 1.0
                )
            weight = weight_ref[pl.ds(row, 1), :]
            score_ref[row] = (weight * (total - pair_sum / member_n)).astype(jnp.bfloat16)
        term_ref[:, 0:channels] += lax.dot_general(
            joined(score_ref, step), joined(block_ref, step), (((1,), (1,)), ((), ())),
            preferred_element_type=jnp.float32,
        )
        return carry

    lax.fori_loop(0, steps, score_step, 0)

    def grad_step(step, carry):
        grad = jnp.dot(
            dec_ref[...], joined(score_ref, step), preferred_element_type=jnp.float32
        ).astype(jnp.bfloat16)
        for r in range(rows_at_once):
            grad_ref[step * rows_at_once + r] = grad[:, r * lat_len : (r + 1) * lat_len]
        return carry

    per = mine_sum.shape[0]
    tall = term_ref.shape[0] // 8
    across = term_ref.shape[1] // 128
    for a in range(tall):
        for b in range(across):
            at = a * across + b
            mine[at // per, at % per] = (
                scale * term_ref[8 * a : 8 * a + 8, 128 * b : 128 * b + 128]
            )
    for at in range(tall * across, n * per):
        mine[at // per, at % per] = jnp.zeros((8, 128), jnp.float32)

    def scatter_copy(e):
        other, device = peer(e)
        return pltpu.make_async_remote_copy(
            src_ref=mine.at[other], dst_ref=got.at[e], send_sem=sems.at[0, e],
            recv_sem=sems.at[1, e], device_id=device, device_id_type=MESH,
        )

    def gather_copy(e):
        _, device = peer(e)
        return pltpu.make_async_remote_copy(
            src_ref=mine_sum, dst_ref=whole.at[e], send_sem=sems.at[2, e],
            recv_sem=sems.at[3, e], device_id=device, device_id_type=MESH,
        )

    def start(make):
        def body(e, carry):
            make(e).start()
            return carry

        lax.fori_loop(0, n - 1, body, 0)

    def finish(make):
        def body(e, carry):
            make(e).wait()
            return carry

        lax.fori_loop(0, n - 1, body, 0)

    start(scatter_copy)
    lax.fori_loop(0, steps // 2, grad_step, 0)
    finish(scatter_copy)
    total = mine[me]
    for e in range(n - 1):
        total = total + got[e]
    mine_sum[...] = total
    start(gather_copy)
    out_ref[me] = total
    lax.fori_loop(steps // 2, steps, grad_step, 0)
    finish(gather_copy)
    for e in range(n - 1):
        out_ref[lax.rem(me + n - e - 1, n)] = whole[e]


def per_device(features, depth_kernel, in_weight, out_weight, decoder_weight, observed, land_mask):
    _, channels, lon_len, lat_len = features.shape
    outputs = decoder_weight.shape[1]
    size = depth_kernel.shape[1]
    half = size // 2
    member_n = lax.axis_size("member")
    space_n = lax.axis_size("space")
    n = member_n * space_n
    members = features.shape[0] * member_n
    total_points = lon_len * space_n * lat_len
    padded_c = round_up(channels, 16)

    x = jnp.transpose(features[0], (1, 0, 2))
    forth = [(i, (i + 1) % space_n) for i in range(space_n)]
    back = [((i + 1) % space_n, i) for i in range(space_n)]
    left = lax.ppermute(x[lon_len - half :], "space", forth)
    right = lax.ppermute(x[:half], "space", back)
    taps = jnp.pad(depth_kernel.reshape(channels, size * size), ((0, padded_c - channels), (0, 0)))
    normed = pl.pallas_call(
        conv_kernel,
        name="conv",
        out_shape=jax.ShapeDtypeStruct((lon_len, channels, lat_len), jnp.bfloat16),
        in_specs=[VMEM_SPEC] * 4,
        out_specs=VMEM_SPEC,
        scratch_shapes=[
            pltpu.VMEM((lon_len, padded_c, lat_len), jnp.float32),
            pltpu.VMEM((lon_len, 8, lat_len), jnp.float32),
            pltpu.VMEM((lon_len + 2 * half, 16, lat_len), jnp.float32),
        ],
    )(x, left, right, taps)
    weight = 4.0 + 8.0 * land_mask.astype(jnp.float32)
    wide_c = round_up(channels, 128)
    tiles = (outputs // 8) * (wide_c // 128)
    per = -(-tiles // n)
    rows_at_once = 2
    grad, summed = pl.pallas_call(
        functools.partial(
            main_kernel, (member_n, space_n), rows_at_once, 1.0 / math.sqrt(members * total_points)
        ),
        name="main",
        out_shape=(
            jax.ShapeDtypeStruct((lon_len, channels, lat_len), jnp.bfloat16),
            jax.ShapeDtypeStruct((n, per, 8, 128), jnp.float32),
        ),
        in_specs=[VMEM_SPEC] * 8,
        out_specs=[VMEM_SPEC] * 2,
        scratch_shapes=[
            pltpu.VMEM((lon_len, channels, lat_len), jnp.bfloat16),
            pltpu.VMEM((lon_len, outputs, lat_len), jnp.bfloat16),
            pltpu.VMEM((member_n - 1, lon_len, outputs, lat_len), jnp.bfloat16),
            pltpu.VMEM((lon_len, outputs, lat_len), jnp.bfloat16),
            pltpu.VMEM((outputs, wide_c), jnp.float32),
            pltpu.VMEM((n, per, 8, 128), jnp.float32),
            pltpu.VMEM((n - 1, per, 8, 128), jnp.float32),
            pltpu.VMEM((per, 8, 128), jnp.float32),
            pltpu.VMEM((n - 1, per, 8, 128), jnp.float32),
            pltpu.SemaphoreType.DMA((2, member_n - 1, lon_len // rows_at_once)),
            pltpu.SemaphoreType.DMA((4, n - 1)),
        ],
        compiler_params=pltpu.CompilerParams(collective_id=0, has_side_effects=True),
    )(
        x, normed, in_weight.T, out_weight.T, decoder_weight.T, decoder_weight,
        jnp.transpose(observed, (1, 0, 2)), weight,
    )
    flat = summed.reshape(n * per, 8, 128)[:tiles].reshape(outputs // 8, wide_c // 128, 8, 128)
    decoder_grad = jnp.transpose(flat, (0, 2, 1, 3)).reshape(outputs, wide_c)[:, :channels].T
    grad_features = jnp.transpose(grad, (1, 0, 2))[None]
    return (grad_features, decoder_grad)


def solution(mesh):
    placed = (
        P("member", None, "space", None),
        P(),
        P(),
        P(),
        P(),
        P(None, "space", None),
        P("space", None),
    )
    return jax.shard_map(
        per_device,
        mesh=mesh,
        in_specs=placed,
        out_specs=(P("member", None, "space", None), P()),
        check_vma=False,
    )
```

```python
import functools
import math

import jax
import jax.numpy as jnp
from jax import lax
from jax.experimental import pallas as pl
from jax.experimental.pallas import tpu as pltpu
from jax.sharding import PartitionSpec as P

norm_eps = 1e-05
MESH = pl.DeviceIdType.MESH
VMEM_SPEC = pl.BlockSpec(memory_space=pltpu.VMEM)


def round_up(value, step):
    return -(-value // step) * step


def gelu(x):
    return 0.5 * x * (1.0 + lax.erf(x * (0.5**0.5)))


def conv_kernel(segments, *refs):
    sources = refs[: len(segments)]
    taps_ref, normed_ref, conv_ref, wide_ref = refs[len(segments) :]
    channels, lat_len = sources[0].shape[1:]
    rows_out = conv_ref.shape[0]
    size = math.isqrt(taps_ref.shape[1])
    half = size // 2
    full = channels // 16
    rest = channels - full * 16
    lane = lax.broadcasted_iota(jnp.int32, (8, lat_len), 1)
    runs = []
    at = 0
    for group in sorted(set(segments)):
        count = sum(r.shape[0] for r, g in zip(sources, segments) if g == group)
        runs.append((at, count))
        at += count

    def fill(chan, kept):
        at = 0
        for ref in sources:
            for i in range(ref.shape[0]):
                wide_ref[at, 0:kept, :] = ref[i, chan, :].astype(jnp.float32)
                at += 1

    def convolve(first):
        for part8 in range(2):
            sub = slice(part8 * 8, part8 * 8 + 8)
            chan = pl.ds(pl.multiple_of(first + part8 * 8, 8), 8)
            coef = [
                jnp.broadcast_to(taps_ref[chan, t : t + 1], (8, lat_len))
                for t in range(size * size)
            ]
            row = 0
            for begin, count in runs:
                for i in range(begin, begin + count - 2 * half):
                    cells = [wide_ref[i + p, sub, :] for p in range(size)]
                    total = None
                    for q in range(size):
                        part = coef[q] * cells[0]
                        for p in range(1, size):
                            part = part + coef[p * size + q] * cells[p]
                        shift = half - q
                        if shift != 0:
                            part = pltpu.roll(part, shift % lat_len, 1)
                            inside = lane >= shift if shift > 0 else lane < lat_len + shift
                            part = jnp.where(inside, part, 0.0)
                        total = part if total is None else total + part
                    conv_ref[row, chan, :] = total
                    row += 1

    def conv_block(block, carry):
        first = pl.multiple_of(block * 16, 16)
        fill(pl.ds(first, 16), 16)
        convolve(first)
        return carry

    lax.fori_loop(0, full, conv_block, 0)
    if rest > 0:
        wide_ref[...] = jnp.zeros_like(wide_ref)
        fill(slice(full * 16, channels), rest)
        convolve(full * 16)

    def norm_row(row, carry):
        cells = conv_ref[row, 0:channels, :]
        shifted = cells - jnp.sum(cells, axis=0, keepdims=True) * (1.0 / channels)
        square = jnp.sum(shifted * shifted, axis=0, keepdims=True)
        scale = lax.rsqrt(square * (1.0 / channels) + norm_eps)
        normed_ref[row] = (shifted * scale).astype(jnp.bfloat16)
        return carry

    lax.fori_loop(0, rows_out, norm_row, 0)


def conv_norm(name, half, segments, sources, taps):
    channels, lat_len = sources[0].shape[1:]
    rows_in = sum(part.shape[0] for part in sources)
    rows_out = rows_in - 2 * half * len(set(segments))
    padded_c = taps.shape[0]
    return pl.pallas_call(
        functools.partial(conv_kernel, segments),
        name=name,
        out_shape=jax.ShapeDtypeStruct((rows_out, channels, lat_len), jnp.bfloat16),
        in_specs=[VMEM_SPEC] * (len(sources) + 1),
        out_specs=VMEM_SPEC,
        scratch_shapes=[
            pltpu.VMEM((rows_out, padded_c, lat_len), jnp.float32),
            pltpu.VMEM((rows_in, 16, lat_len), jnp.float32),
        ],
        cost_estimate=pl.CostEstimate(
            flops=2000 * rows_out * channels * lat_len,
            bytes_accessed=4 * rows_in * channels * lat_len,
            transcendentals=0,
        ),
    )(*sources, taps)


def cuts_of(hid):
    width = round_up(-(-hid // 3), 256)
    return [(at, min(at + width, hid)) for at in range(0, hid, width)]


def main_kernel(
    groups, rows_at_once, scale, x_ref, inner_ref, edge_ref, w1_ref, w2_ref, dect_ref, dec_ref, observed_ref,
    weight_ref, grad_ref, out_ref, block_ref, own_ref, others_ref, score_ref, term_ref, tall_ref, mine, got,
    mine_sum, whole, pair_sems, sems,
):
    lon_len, channels, lat_len = x_ref.shape
    member_n, space_n = groups
    n = member_n * space_n
    member = lax.axis_index("member")
    space = lax.axis_index("space")
    me = member * space_n + space
    steps = lon_len // rows_at_once

    def peer(e):
        other = lax.rem(me + e + 1, n)
        return other, (other // space_n, lax.rem(other, space_n))

    barrier = pltpu.get_barrier_semaphore()

    def greet(e, carry):
        pl.semaphore_signal(barrier, inc=1, device_id=peer(e)[1], device_id_type=MESH)
        return carry

    lax.fori_loop(0, n - 1, greet, 0)

    def joined(ref, step):
        return jnp.concatenate([ref[step * rows_at_once + r] for r in range(rows_at_once)], axis=1)

    def mlp_step(step, normed_ref, at):
        normed = joined(normed_ref, at)
        out = joined(x_ref, step).astype(jnp.float32)
        for low, high in cuts_of(w1_ref.shape[0]):
            pre = jnp.dot(w1_ref[low:high, :], normed, preferred_element_type=jnp.float32)
            act = gelu(pre).astype(jnp.bfloat16)
            out = out + jnp.dot(w2_ref[:, low:high], act, preferred_element_type=jnp.float32)
        block_out = out.astype(jnp.bfloat16)
        decoded = jnp.dot(dect_ref[...], block_out, preferred_element_type=jnp.float32).astype(
            jnp.bfloat16
        )
        for r in range(rows_at_once):
            cols = slice(r * lat_len, (r + 1) * lat_len)
            block_ref[step * rows_at_once + r] = block_out[:, cols]
            own_ref[step * rows_at_once + r] = decoded[:, cols]

    def pair_copy(step, j):
        rows = pl.ds(step * rows_at_once, rows_at_once)
        return pltpu.make_async_remote_copy(
            src_ref=own_ref.at[rows], dst_ref=others_ref.at[j, rows],
            send_sem=pair_sems.at[0, j, step], recv_sem=pair_sems.at[1, j, step],
            device_id=(lax.rem(member + j + 1, member_n), space), device_id_type=MESH,
        )

    mlp_step(0, edge_ref, 0)
    pl.semaphore_wait(barrier, n - 1)
    for j in range(member_n - 1):
        pair_copy(0, j).start()

    def mlp_loop(step, carry):
        mlp_step(step, inner_ref, step - 1)
        for j in range(member_n - 1):
            pair_copy(step, j).start()
        return carry

    lax.fori_loop(1, steps - 1, mlp_loop, 0)
    mlp_step(steps - 1, edge_ref, 1)
    for j in range(member_n - 1):
        pair_copy(steps - 1, j).start()
    term_ref[...] = jnp.zeros_like(term_ref)
    tall_ref[...] = jnp.zeros_like(tall_ref)

    def score_step(step, carry):
        for j in range(member_n - 1):
            pair_copy(step, j).wait()
        for r in range(rows_at_once):
            row = step * rows_at_once + r
            own = own_ref[row].astype(jnp.float32)
            misfit = own - observed_ref[row]
            total = misfit * lax.rsqrt(jnp.sum(misfit * misfit, axis=0, keepdims=True) + 1.0)
            pair_sum = jnp.zeros_like(own)
            for k in range(member_n):
                other = own_ref[row] if k == member_n - 1 else others_ref[k, row]
                apart = own - other.astype(jnp.float32)
                pair_sum = pair_sum + apart * lax.rsqrt(
                    jnp.sum(apart * apart, axis=0, keepdims=True) + 1.0
                )
            weight = weight_ref[pl.ds(row, 1), :]
            score_ref[row] = (weight * (total - pair_sum / member_n)).astype(jnp.bfloat16)
        tall_ref[...] += lax.dot_general(
            joined(block_ref, step), joined(score_ref, step), (((1,), (1,)), ((), ())),
            preferred_element_type=jnp.float32,
        )
        return carry

    lax.fori_loop(0, steps, score_step, 0)
    term_ref[:, 0:channels] = scale * jnp.transpose(tall_ref[...])

    def grad_step(step, carry):
        grad = jnp.dot(
            dec_ref[...], joined(score_ref, step), preferred_element_type=jnp.float32
        ).astype(jnp.bfloat16)
        for r in range(rows_at_once):
            grad_ref[step * rows_at_once + r] = grad[:, r * lat_len : (r + 1) * lat_len]
        return carry

    per = mine_sum.shape[0] // 8
    tall = term_ref.shape[0] // 8
    across = term_ref.shape[1] // 128
    for a in range(tall):
        for b in range(across):
            at = a * across + b
            low = 8 * (at % per)
            mine[at // per, low : low + 8, :] = term_ref[
                8 * a : 8 * a + 8, 128 * b : 128 * b + 128
            ].astype(jnp.bfloat16)
    for at in range(tall * across, n * per):
        low = 8 * (at % per)
        mine[at // per, low : low + 8, :] = jnp.zeros((8, 128), jnp.bfloat16)

    def scatter_copy(e):
        other, device = peer(e)
        return pltpu.make_async_remote_copy(
            src_ref=mine.at[other], dst_ref=got.at[e], send_sem=sems.at[0, e],
            recv_sem=sems.at[1, e], device_id=device, device_id_type=MESH,
        )

    def gather_copy(e):
        _, device = peer(e)
        return pltpu.make_async_remote_copy(
            src_ref=mine_sum, dst_ref=whole.at[e], send_sem=sems.at[2, e],
            recv_sem=sems.at[3, e], device_id=device, device_id_type=MESH,
        )

    def start(make):
        def body(e, carry):
            make(e).start()
            return carry

        lax.fori_loop(0, n - 1, body, 0)

    def finish(make):
        def body(e, carry):
            make(e).wait()
            return carry

        lax.fori_loop(0, n - 1, body, 0)

    start(scatter_copy)
    lax.fori_loop(0, steps // 2, grad_step, 0)
    finish(scatter_copy)
    total = mine[me].astype(jnp.float32)
    for e in range(n - 1):
        total = total + got[e].astype(jnp.float32)
    mine_sum[...] = total
    start(gather_copy)
    out_ref[me] = total
    lax.fori_loop(steps // 2, steps, grad_step, 0)
    finish(gather_copy)
    for e in range(n - 1):
        out_ref[lax.rem(me + n - e - 1, n)] = whole[e]


def per_device(features, depth_kernel, in_weight, out_weight, decoder_weight, observed, land_mask):
    _, channels, lon_len, lat_len = features.shape
    outputs = decoder_weight.shape[1]
    size = depth_kernel.shape[1]
    half = size // 2
    member_n = lax.axis_size("member")
    space_n = lax.axis_size("space")
    n = member_n * space_n
    members = features.shape[0] * member_n
    total_points = lon_len * space_n * lat_len
    padded_c = round_up(channels, 16)

    x = jnp.transpose(features[0], (1, 0, 2))
    forth = [(i, (i + 1) % space_n) for i in range(space_n)]
    back = [((i + 1) % space_n, i) for i in range(space_n)]
    left = lax.ppermute(x[lon_len - half :], "space", forth)
    right = lax.ppermute(x[:half], "space", back)
    taps = jnp.pad(depth_kernel.reshape(channels, size * size), ((0, padded_c - channels), (0, 0)))
    inner = conv_norm("inner", half, (0,), (x,), taps)
    edge = conv_norm(
        "edge", half, (0, 0, 1, 1), (left, x[: 2 * half], x[lon_len - 2 * half :], right), taps
    )
    weight = 4.0 + 8.0 * land_mask.astype(jnp.float32)
    wide_c = round_up(channels, 128)
    tiles = (outputs // 8) * (wide_c // 128)
    per = -(-tiles // n)
    rows_at_once = half
    grad, summed = pl.pallas_call(
        functools.partial(
            main_kernel, (member_n, space_n), rows_at_once, 1.0 / math.sqrt(members * total_points)
        ),
        name="main",
        out_shape=(
            jax.ShapeDtypeStruct((lon_len, channels, lat_len), jnp.bfloat16),
            jax.ShapeDtypeStruct((n, per * 8, 128), jnp.float32),
        ),
        in_specs=[VMEM_SPEC] * 9,
        out_specs=[VMEM_SPEC] * 2,
        scratch_shapes=[
            pltpu.VMEM((lon_len, channels, lat_len), jnp.bfloat16),
            pltpu.VMEM((lon_len, outputs, lat_len), jnp.bfloat16),
            pltpu.VMEM((member_n - 1, lon_len, outputs, lat_len), jnp.bfloat16),
            pltpu.VMEM((lon_len, outputs, lat_len), jnp.bfloat16),
            pltpu.VMEM((outputs, wide_c), jnp.float32),
            pltpu.VMEM((channels, outputs), jnp.float32),
            pltpu.VMEM((n, per * 8, 128), jnp.bfloat16),
            pltpu.VMEM((n - 1, per * 8, 128), jnp.bfloat16),
            pltpu.VMEM((per * 8, 128), jnp.float32),
            pltpu.VMEM((n - 1, per * 8, 128), jnp.float32),
            pltpu.SemaphoreType.DMA((2, member_n - 1, lon_len // rows_at_once)),
            pltpu.SemaphoreType.DMA((4, n - 1)),
        ],
        compiler_params=pltpu.CompilerParams(collective_id=0, has_side_effects=True),
    )(
        x, inner, edge, in_weight.T, out_weight.T, decoder_weight.T, decoder_weight,
        jnp.transpose(observed, (1, 0, 2)), weight,
    )
    flat = summed.reshape(n * per, 8, 128)[:tiles].reshape(outputs // 8, wide_c // 128, 8, 128)
    decoder_grad = jnp.transpose(flat, (0, 2, 1, 3)).reshape(outputs, wide_c)[:, :channels].T
    grad_features = jnp.transpose(grad, (1, 0, 2))[None]
    return (grad_features, decoder_grad)


def solution(mesh):
    placed = (
        P("member", None, "space", None),
        P(),
        P(),
        P(),
        P(),
        P(None, "space", None),
        P("space", None),
    )
    return jax.shard_map(
        per_device,
        mesh=mesh,
        in_specs=placed,
        out_specs=(P("member", None, "space", None), P()),
        check_vma=False,
    )
```

```python
import functools
import math

import jax
import jax.numpy as jnp
from jax import lax
from jax.experimental import pallas as pl
from jax.experimental.pallas import tpu as pltpu
from jax.sharding import PartitionSpec as P

norm_eps = 1e-05
MESH = pl.DeviceIdType.MESH
VMEM_SPEC = pl.BlockSpec(memory_space=pltpu.VMEM)


def round_up(value, step):
    return -(-value // step) * step


def gelu(x):
    return 0.5 * x * (1.0 + lax.erf(x * (0.5**0.5)))


def conv_kernel(segments, *refs):
    sources = refs[: len(segments)]
    taps_ref, normed_ref, conv_ref, wide_ref, spread_ref = refs[len(segments) :]
    channels, lat_len = sources[0].shape[1:]
    rows_out = conv_ref.shape[0]
    count_taps = taps_ref.shape[1] // 3
    size = math.isqrt(count_taps)
    half = size // 2
    full = channels // 16
    rest = channels - full * 16
    lane = lax.broadcasted_iota(jnp.int32, (8, lat_len), 1)
    taps = taps_ref[...]
    high = taps.astype(jnp.bfloat16).astype(jnp.float32)
    middle = (taps - high).astype(jnp.bfloat16).astype(jnp.float32)
    low = taps - high - middle
    column = lax.broadcasted_iota(jnp.int32, taps.shape, 1)
    parts = jnp.where(
        column < count_taps, high, jnp.where(column < 2 * count_taps, middle, low)
    ).astype(jnp.bfloat16)
    for t in range(count_taps):
        at_row = lax.broadcasted_iota(jnp.int32, (3 * count_taps, lat_len), 0)
        chosen = (at_row == t) | (at_row == t + count_taps) | (at_row == t + 2 * count_taps)
        spread_ref[t] = jnp.dot(
            parts, jnp.where(chosen, 1.0, 0.0).astype(jnp.bfloat16),
            preferred_element_type=jnp.float32,
        )
    runs = []
    at = 0
    for group in sorted(set(segments)):
        count = sum(r.shape[0] for r, g in zip(sources, segments) if g == group)
        runs.append((at, count))
        at += count

    def fill(chan, kept):
        at = 0
        for ref in sources:
            for i in range(ref.shape[0]):
                wide_ref[at, 0:kept, :] = ref[i, chan, :].astype(jnp.float32)
                at += 1

    def convolve(first):
        for part8 in range(2):
            sub = slice(part8 * 8, part8 * 8 + 8)
            chan = pl.ds(pl.multiple_of(first + part8 * 8, 8), 8)
            coef = [spread_ref[t, chan, :] for t in range(size * size)]
            row = 0
            for begin, count in runs:
                for i in range(begin, begin + count - 2 * half):
                    cells = [wide_ref[i + p, sub, :] for p in range(size)]
                    total = None
                    for q in range(size):
                        part = coef[q] * cells[0]
                        for p in range(1, size):
                            part = part + coef[p * size + q] * cells[p]
                        shift = half - q
                        if shift != 0:
                            part = pltpu.roll(part, shift % lat_len, 1)
                            inside = lane >= shift if shift > 0 else lane < lat_len + shift
                            part = jnp.where(inside, part, 0.0)
                        total = part if total is None else total + part
                    conv_ref[row, chan, :] = total
                    row += 1

    def conv_block(block, carry):
        first = pl.multiple_of(block * 16, 16)
        fill(pl.ds(first, 16), 16)
        convolve(first)
        return carry

    lax.fori_loop(0, full, conv_block, 0)
    if rest > 0:
        wide_ref[...] = jnp.zeros_like(wide_ref)
        fill(slice(full * 16, channels), rest)
        convolve(full * 16)

    def norm_row(row, carry):
        cells = conv_ref[row, 0:channels, :]
        shifted = cells - jnp.sum(cells, axis=0, keepdims=True) * (1.0 / channels)
        square = jnp.sum(shifted * shifted, axis=0, keepdims=True)
        scale = lax.rsqrt(square * (1.0 / channels) + norm_eps)
        normed_ref[row] = (shifted * scale).astype(jnp.bfloat16)
        return carry

    lax.fori_loop(0, rows_out, norm_row, 0)


def conv_norm(name, half, segments, sources, taps):
    channels, lat_len = sources[0].shape[1:]
    rows_in = sum(part.shape[0] for part in sources)
    rows_out = rows_in - 2 * half * len(set(segments))
    padded_c = taps.shape[0]
    return pl.pallas_call(
        functools.partial(conv_kernel, segments),
        name=name,
        out_shape=jax.ShapeDtypeStruct((rows_out, channels, lat_len), jnp.bfloat16),
        in_specs=[VMEM_SPEC] * (len(sources) + 1),
        out_specs=VMEM_SPEC,
        scratch_shapes=[
            pltpu.VMEM((rows_out, padded_c, lat_len), jnp.float32),
            pltpu.VMEM((rows_in, 16, lat_len), jnp.float32),
            pltpu.VMEM((taps.shape[1] // 3, padded_c, lat_len), jnp.float32),
        ],
        cost_estimate=pl.CostEstimate(
            flops=2000 * rows_out * channels * lat_len,
            bytes_accessed=4 * rows_in * channels * lat_len,
            transcendentals=0,
        ),
    )(*sources, taps)


def cuts_of(hid):
    width = round_up(-(-hid // 3), 256)
    return [(at, min(at + width, hid)) for at in range(0, hid, width)]


def main_kernel(
    groups, rows_at_once, scale, x_ref, inner_ref, edge_ref, w1_ref, w2_ref, dect_ref, dec_ref, observed_ref,
    weight_ref, grad_ref, out_ref, block_ref, own_ref, others_ref, score_ref, term_ref, tall_ref, mine, got,
    mine_sum, whole, pair_sems, sems,
):
    lon_len, channels, lat_len = x_ref.shape
    member_n, space_n = groups
    n = member_n * space_n
    member = lax.axis_index("member")
    space = lax.axis_index("space")
    me = member * space_n + space
    steps = lon_len // rows_at_once

    def peer(e):
        other = lax.rem(me + e + 1, n)
        return other, (other // space_n, lax.rem(other, space_n))

    barrier = pltpu.get_barrier_semaphore()

    def greet(e, carry):
        pl.semaphore_signal(barrier, inc=1, device_id=peer(e)[1], device_id_type=MESH)
        return carry

    lax.fori_loop(0, n - 1, greet, 0)

    def joined(ref, step):
        return jnp.concatenate([ref[step * rows_at_once + r] for r in range(rows_at_once)], axis=1)

    def mlp_step(step, normed_ref, at):
        normed = joined(normed_ref, at)
        out = joined(x_ref, step).astype(jnp.float32)
        for low, high in cuts_of(w1_ref.shape[0]):
            pre = jnp.dot(w1_ref[low:high, :], normed, preferred_element_type=jnp.float32)
            act = gelu(pre).astype(jnp.bfloat16)
            out = out + jnp.dot(w2_ref[:, low:high], act, preferred_element_type=jnp.float32)
        block_out = out.astype(jnp.bfloat16)
        decoded = jnp.dot(dect_ref[...], block_out, preferred_element_type=jnp.float32).astype(
            jnp.bfloat16
        )
        for r in range(rows_at_once):
            cols = slice(r * lat_len, (r + 1) * lat_len)
            block_ref[step * rows_at_once + r] = block_out[:, cols]
            own_ref[step * rows_at_once + r] = decoded[:, cols]

    def pair_copy(step, j):
        rows = pl.ds(step * rows_at_once, rows_at_once)
        return pltpu.make_async_remote_copy(
            src_ref=own_ref.at[rows], dst_ref=others_ref.at[j, rows],
            send_sem=pair_sems.at[0, j, step], recv_sem=pair_sems.at[1, j, step],
            device_id=(lax.rem(member + j + 1, member_n), space), device_id_type=MESH,
        )

    mlp_step(0, edge_ref, 0)
    pl.semaphore_wait(barrier, n - 1)
    for j in range(member_n - 1):
        pair_copy(0, j).start()

    def mlp_loop(step, carry):
        mlp_step(step, inner_ref, step - 1)
        for j in range(member_n - 1):
            pair_copy(step, j).start()
        return carry

    lax.fori_loop(1, steps - 1, mlp_loop, 0)
    mlp_step(steps - 1, edge_ref, 1)
    for j in range(member_n - 1):
        pair_copy(steps - 1, j).start()
    term_ref[...] = jnp.zeros_like(term_ref)
    tall_ref[...] = jnp.zeros_like(tall_ref)

    def score_step(step, carry):
        for j in range(member_n - 1):
            pair_copy(step, j).wait()
        for r in range(rows_at_once):
            row = step * rows_at_once + r
            own = own_ref[row].astype(jnp.float32)
            misfit = own - observed_ref[row]
            total = misfit * lax.rsqrt(jnp.sum(misfit * misfit, axis=0, keepdims=True) + 1.0)
            pair_sum = jnp.zeros_like(own)
            for k in range(member_n):
                other = own_ref[row] if k == member_n - 1 else others_ref[k, row]
                apart = own - other.astype(jnp.float32)
                pair_sum = pair_sum + apart * lax.rsqrt(
                    jnp.sum(apart * apart, axis=0, keepdims=True) + 1.0
                )
            weight = weight_ref[pl.ds(row, 1), :]
            score_ref[row] = (weight * (total - pair_sum / member_n)).astype(jnp.bfloat16)
        tall_ref[...] += lax.dot_general(
            joined(block_ref, step), joined(score_ref, step), (((1,), (1,)), ((), ())),
            preferred_element_type=jnp.float32,
        )
        return carry

    lax.fori_loop(0, steps, score_step, 0)
    term_ref[:, 0:channels] = scale * jnp.transpose(tall_ref[...])

    def grad_step(step, carry):
        grad = jnp.dot(
            dec_ref[...], joined(score_ref, step), preferred_element_type=jnp.float32
        ).astype(jnp.bfloat16)
        for r in range(rows_at_once):
            grad_ref[step * rows_at_once + r] = grad[:, r * lat_len : (r + 1) * lat_len]
        return carry

    per = mine_sum.shape[0] // 8
    tall = term_ref.shape[0] // 8
    across = term_ref.shape[1] // 128
    for a in range(tall):
        for b in range(across):
            at = a * across + b
            low = 8 * (at % per)
            mine[at // per, low : low + 8, :] = term_ref[
                8 * a : 8 * a + 8, 128 * b : 128 * b + 128
            ].astype(jnp.bfloat16)
    for at in range(tall * across, n * per):
        low = 8 * (at % per)
        mine[at // per, low : low + 8, :] = jnp.zeros((8, 128), jnp.bfloat16)

    def scatter_copy(e):
        other, device = peer(e)
        return pltpu.make_async_remote_copy(
            src_ref=mine.at[other], dst_ref=got.at[e], send_sem=sems.at[0, e],
            recv_sem=sems.at[1, e], device_id=device, device_id_type=MESH,
        )

    def gather_copy(e):
        _, device = peer(e)
        return pltpu.make_async_remote_copy(
            src_ref=mine_sum, dst_ref=whole.at[e], send_sem=sems.at[2, e],
            recv_sem=sems.at[3, e], device_id=device, device_id_type=MESH,
        )

    def start(make):
        def body(e, carry):
            make(e).start()
            return carry

        lax.fori_loop(0, n - 1, body, 0)

    def finish(make):
        def body(e, carry):
            make(e).wait()
            return carry

        lax.fori_loop(0, n - 1, body, 0)

    start(scatter_copy)
    lax.fori_loop(0, steps // 2, grad_step, 0)
    finish(scatter_copy)
    total = mine[me].astype(jnp.float32)
    for e in range(n - 1):
        total = total + got[e].astype(jnp.float32)
    mine_sum[...] = total.astype(jnp.bfloat16)
    start(gather_copy)
    out_ref[me] = mine_sum[...].astype(jnp.float32)
    lax.fori_loop(steps // 2, steps, grad_step, 0)
    finish(gather_copy)
    for e in range(n - 1):
        out_ref[lax.rem(me + n - e - 1, n)] = whole[e].astype(jnp.float32)


def per_device(features, depth_kernel, in_weight, out_weight, decoder_weight, observed, land_mask):
    _, channels, lon_len, lat_len = features.shape
    outputs = decoder_weight.shape[1]
    size = depth_kernel.shape[1]
    half = size // 2
    member_n = lax.axis_size("member")
    space_n = lax.axis_size("space")
    n = member_n * space_n
    members = features.shape[0] * member_n
    total_points = lon_len * space_n * lat_len
    padded_c = round_up(channels, 16)

    x = jnp.transpose(features[0], (1, 0, 2))
    forth = [(i, (i + 1) % space_n) for i in range(space_n)]
    back = [((i + 1) % space_n, i) for i in range(space_n)]
    left = lax.ppermute(x[lon_len - half :], "space", forth)
    right = lax.ppermute(x[:half], "space", back)
    taps = jnp.pad(depth_kernel.reshape(channels, size * size), ((0, padded_c - channels), (0, 0)))
    taps = jnp.concatenate([taps, taps, taps], axis=1)
    inner = conv_norm("inner", half, (0,), (x,), taps)
    edge = conv_norm(
        "edge", half, (0, 0, 1, 1), (left, x[: 2 * half], x[lon_len - 2 * half :], right), taps
    )
    weight = 4.0 + 8.0 * land_mask.astype(jnp.float32)
    wide_c = round_up(channels, 128)
    tiles = (outputs // 8) * (wide_c // 128)
    per = -(-tiles // n)
    rows_at_once = half
    grad, summed = pl.pallas_call(
        functools.partial(
            main_kernel, (member_n, space_n), rows_at_once, 1.0 / math.sqrt(members * total_points)
        ),
        name="main",
        out_shape=(
            jax.ShapeDtypeStruct((lon_len, channels, lat_len), jnp.bfloat16),
            jax.ShapeDtypeStruct((n, per * 8, 128), jnp.float32),
        ),
        in_specs=[VMEM_SPEC] * 9,
        out_specs=[VMEM_SPEC] * 2,
        scratch_shapes=[
            pltpu.VMEM((lon_len, channels, lat_len), jnp.bfloat16),
            pltpu.VMEM((lon_len, outputs, lat_len), jnp.bfloat16),
            pltpu.VMEM((member_n - 1, lon_len, outputs, lat_len), jnp.bfloat16),
            pltpu.VMEM((lon_len, outputs, lat_len), jnp.bfloat16),
            pltpu.VMEM((outputs, wide_c), jnp.float32),
            pltpu.VMEM((channels, outputs), jnp.float32),
            pltpu.VMEM((n, per * 8, 128), jnp.bfloat16),
            pltpu.VMEM((n - 1, per * 8, 128), jnp.bfloat16),
            pltpu.VMEM((per * 8, 128), jnp.bfloat16),
            pltpu.VMEM((n - 1, per * 8, 128), jnp.bfloat16),
            pltpu.SemaphoreType.DMA((2, member_n - 1, lon_len // rows_at_once)),
            pltpu.SemaphoreType.DMA((4, n - 1)),
        ],
        compiler_params=pltpu.CompilerParams(collective_id=0, has_side_effects=True),
    )(
        x, inner, edge, in_weight.T, out_weight.T, decoder_weight.T, decoder_weight,
        jnp.transpose(observed, (1, 0, 2)), weight,
    )
    flat = summed.reshape(n * per, 8, 128)[:tiles].reshape(outputs // 8, wide_c // 128, 8, 128)
    decoder_grad = jnp.transpose(flat, (0, 2, 1, 3)).reshape(outputs, wide_c)[:, :channels].T
    grad_features = jnp.transpose(grad, (1, 0, 2))[None]
    return (grad_features, decoder_grad)


def solution(mesh):
    placed = (
        P("member", None, "space", None),
        P(),
        P(),
        P(),
        P(),
        P(None, "space", None),
        P("space", None),
    )
    return jax.shard_map(
        per_device,
        mesh=mesh,
        in_specs=placed,
        out_specs=(P("member", None, "space", None), P()),
        check_vma=False,
    )
```

```python
import functools
import math

import jax
import jax.numpy as jnp
from jax import lax
from jax.experimental import pallas as pl
from jax.experimental.pallas import tpu as pltpu
from jax.sharding import PartitionSpec as P

norm_eps = 1e-05
MESH = pl.DeviceIdType.MESH
VMEM_SPEC = pl.BlockSpec(memory_space=pltpu.VMEM)


def round_up(value, step):
    return -(-value // step) * step


def gelu(x):
    return 0.5 * x * (1.0 + lax.erf(x * (0.5**0.5)))


def conv_kernel(segments, *refs):
    sources = refs[: len(segments)]
    taps_ref, normed_ref, conv_ref, wide_ref, spread_ref = refs[len(segments) :]
    channels, lat_len = sources[0].shape[1:]
    rows_out = conv_ref.shape[0]
    count_taps = taps_ref.shape[1] // 3
    size = math.isqrt(count_taps)
    half = size // 2
    full = channels // 16
    rest = channels - full * 16
    lane = lax.broadcasted_iota(jnp.int32, (8, lat_len), 1)
    taps = taps_ref[...]
    high = taps.astype(jnp.bfloat16).astype(jnp.float32)
    middle = (taps - high).astype(jnp.bfloat16).astype(jnp.float32)
    low = taps - high - middle
    column = lax.broadcasted_iota(jnp.int32, taps.shape, 1)
    parts = jnp.where(
        column < count_taps, high, jnp.where(column < 2 * count_taps, middle, low)
    ).astype(jnp.bfloat16)
    for t in range(count_taps):
        at_row = lax.broadcasted_iota(jnp.int32, (3 * count_taps, lat_len), 0)
        chosen = (at_row == t) | (at_row == t + count_taps) | (at_row == t + 2 * count_taps)
        spread_ref[t] = jnp.dot(
            parts, jnp.where(chosen, 1.0, 0.0).astype(jnp.bfloat16),
            preferred_element_type=jnp.float32,
        )
    runs = []
    at = 0
    for group in sorted(set(segments)):
        count = sum(r.shape[0] for r, g in zip(sources, segments) if g == group)
        runs.append((at, count))
        at += count

    rows_in = wide_ref.shape[0] // 2

    def fill(chan, kept, base):
        at = base
        for ref in sources:
            for i in range(ref.shape[0]):
                wide_ref[at, 0:kept, :] = ref[i, chan, :].astype(jnp.float32)
                at += 1

    def convolve(first, base):
        for part8 in range(2):
            sub = slice(part8 * 8, part8 * 8 + 8)
            chan = pl.ds(pl.multiple_of(first + part8 * 8, 8), 8)
            coef = [spread_ref[t, chan, :] for t in range(size * size)]
            row = 0
            for begin, count in runs:
                for i in range(begin, begin + count - 2 * half):
                    cells = [wide_ref[base + i + p, sub, :] for p in range(size)]
                    total = None
                    for q in range(size):
                        part = coef[q] * cells[0]
                        for p in range(1, size):
                            part = part + coef[p * size + q] * cells[p]
                        shift = half - q
                        if shift != 0:
                            part = pltpu.roll(part, shift % lat_len, 1)
                            inside = lane >= shift if shift > 0 else lane < lat_len + shift
                            part = jnp.where(inside, part, 0.0)
                        total = part if total is None else total + part
                    conv_ref[row, chan, :] = total
                    row += 1

    def conv_blocks(pair, carry):
        firsts = [pl.multiple_of(pair * 32 + 16 * slot, 16) for slot in range(2)]
        for slot in range(2):
            fill(pl.ds(firsts[slot], 16), 16, slot * rows_in)
        for slot in range(2):
            convolve(firsts[slot], slot * rows_in)
        return carry

    lax.fori_loop(0, full // 2, conv_blocks, 0)
    if full % 2:
        fill(slice(full * 16 - 16, full * 16), 16, 0)
        convolve(full * 16 - 16, 0)
    if rest > 0:
        wide_ref[...] = jnp.zeros_like(wide_ref)
        fill(slice(full * 16, channels), rest, 0)
        convolve(full * 16, 0)

    def norm_row(row, carry):
        cells = conv_ref[row, 0:channels, :]
        shifted = cells - jnp.sum(cells, axis=0, keepdims=True) * (1.0 / channels)
        square = jnp.sum(shifted * shifted, axis=0, keepdims=True)
        scale = lax.rsqrt(square * (1.0 / channels) + norm_eps)
        normed_ref[row] = (shifted * scale).astype(jnp.bfloat16)
        return carry

    lax.fori_loop(0, rows_out, norm_row, 0)


def conv_norm(name, half, segments, sources, taps):
    channels, lat_len = sources[0].shape[1:]
    rows_in = sum(part.shape[0] for part in sources)
    rows_out = rows_in - 2 * half * len(set(segments))
    padded_c = taps.shape[0]
    return pl.pallas_call(
        functools.partial(conv_kernel, segments),
        name=name,
        out_shape=jax.ShapeDtypeStruct((rows_out, channels, lat_len), jnp.bfloat16),
        in_specs=[VMEM_SPEC] * (len(sources) + 1),
        out_specs=VMEM_SPEC,
        scratch_shapes=[
            pltpu.VMEM((rows_out, padded_c, lat_len), jnp.float32),
            pltpu.VMEM((2 * rows_in, 16, lat_len), jnp.float32),
            pltpu.VMEM((taps.shape[1] // 3, padded_c, lat_len), jnp.float32),
        ],
        cost_estimate=pl.CostEstimate(
            flops=2000 * rows_out * channels * lat_len,
            bytes_accessed=4 * rows_in * channels * lat_len,
            transcendentals=0,
        ),
    )(*sources, taps)


def cuts_of(hid):
    width = round_up(-(-hid // 3), 256)
    return [(at, min(at + width, hid)) for at in range(0, hid, width)]


def main_kernel(
    groups, rows_at_once, scale, x_ref, inner_ref, edge_ref, w1_ref, w2_ref, dect_ref, dec_ref, observed_ref,
    weight_ref, grad_ref, out_ref, block_ref, own_ref, others_ref, score_ref, term_ref, tall_ref, mine, got,
    mine_sum, whole, pair_sems, sems,
):
    lon_len, channels, lat_len = x_ref.shape
    member_n, space_n = groups
    n = member_n * space_n
    member = lax.axis_index("member")
    space = lax.axis_index("space")
    me = member * space_n + space
    steps = lon_len // rows_at_once

    def peer(e):
        other = lax.rem(me + e + 1, n)
        return other, (other // space_n, lax.rem(other, space_n))

    barrier = pltpu.get_barrier_semaphore()

    def greet(e, carry):
        pl.semaphore_signal(barrier, inc=1, device_id=peer(e)[1], device_id_type=MESH)
        return carry

    lax.fori_loop(0, n - 1, greet, 0)

    def joined(ref, step):
        return jnp.concatenate([ref[step * rows_at_once + r] for r in range(rows_at_once)], axis=1)

    def mlp_step(step, normed_ref, at):
        normed = joined(normed_ref, at)
        out = joined(x_ref, step).astype(jnp.float32)
        for low, high in cuts_of(w1_ref.shape[0]):
            pre = jnp.dot(w1_ref[low:high, :], normed, preferred_element_type=jnp.float32)
            act = gelu(pre).astype(jnp.bfloat16)
            out = out + jnp.dot(w2_ref[:, low:high], act, preferred_element_type=jnp.float32)
        block_out = out.astype(jnp.bfloat16)
        decoded = jnp.dot(dect_ref[...], block_out, preferred_element_type=jnp.float32).astype(
            jnp.bfloat16
        )
        for r in range(rows_at_once):
            cols = slice(r * lat_len, (r + 1) * lat_len)
            block_ref[step * rows_at_once + r] = block_out[:, cols]
            own_ref[step * rows_at_once + r] = decoded[:, cols]

    def pair_copy(step, j):
        rows = pl.ds(step * rows_at_once, rows_at_once)
        return pltpu.make_async_remote_copy(
            src_ref=own_ref.at[rows], dst_ref=others_ref.at[j, rows],
            send_sem=pair_sems.at[0, j, step], recv_sem=pair_sems.at[1, j, step],
            device_id=(lax.rem(member + j + 1, member_n), space), device_id_type=MESH,
        )

    mlp_step(0, edge_ref, 0)
    pl.semaphore_wait(barrier, n - 1)
    for j in range(member_n - 1):
        pair_copy(0, j).start()

    def mlp_loop(step, carry):
        mlp_step(step, inner_ref, step - 1)
        for j in range(member_n - 1):
            pair_copy(step, j).start()
        return carry

    lax.fori_loop(1, steps - 1, mlp_loop, 0)
    mlp_step(steps - 1, edge_ref, 1)
    for j in range(member_n - 1):
        pair_copy(steps - 1, j).start()
    term_ref[...] = jnp.zeros_like(term_ref)
    tall_ref[...] = jnp.zeros_like(tall_ref)

    def score_step(step, carry):
        for j in range(member_n - 1):
            pair_copy(step, j).wait()
        for r in range(rows_at_once):
            row = step * rows_at_once + r
            own = own_ref[row].astype(jnp.float32)
            misfit = own - observed_ref[row]
            total = misfit * lax.rsqrt(jnp.sum(misfit * misfit, axis=0, keepdims=True) + 1.0)
            pair_sum = jnp.zeros_like(own)
            for k in range(member_n):
                other = own_ref[row] if k == member_n - 1 else others_ref[k, row]
                apart = own - other.astype(jnp.float32)
                pair_sum = pair_sum + apart * lax.rsqrt(
                    jnp.sum(apart * apart, axis=0, keepdims=True) + 1.0
                )
            weight = weight_ref[pl.ds(row, 1), :]
            score_ref[row] = (weight * (total - pair_sum / member_n)).astype(jnp.bfloat16)
        tall_ref[...] += lax.dot_general(
            joined(block_ref, step), joined(score_ref, step), (((1,), (1,)), ((), ())),
            preferred_element_type=jnp.float32,
        )
        return carry

    lax.fori_loop(0, steps, score_step, 0)
    term_ref[:, 0:channels] = scale * jnp.transpose(tall_ref[...])

    def grad_step(step, carry):
        grad = jnp.dot(
            dec_ref[...], joined(score_ref, step), preferred_element_type=jnp.float32
        ).astype(jnp.bfloat16)
        for r in range(rows_at_once):
            grad_ref[step * rows_at_once + r] = grad[:, r * lat_len : (r + 1) * lat_len]
        return carry

    per = mine_sum.shape[0] // 8
    tall = term_ref.shape[0] // 8
    across = term_ref.shape[1] // 128
    for a in range(tall):
        for b in range(across):
            at = a * across + b
            low = 8 * (at % per)
            mine[at // per, low : low + 8, :] = term_ref[
                8 * a : 8 * a + 8, 128 * b : 128 * b + 128
            ].astype(jnp.bfloat16)
    for at in range(tall * across, n * per):
        low = 8 * (at % per)
        mine[at // per, low : low + 8, :] = jnp.zeros((8, 128), jnp.bfloat16)

    def scatter_copy(e):
        other, device = peer(e)
        return pltpu.make_async_remote_copy(
            src_ref=mine.at[other], dst_ref=got.at[e], send_sem=sems.at[0, e],
            recv_sem=sems.at[1, e], device_id=device, device_id_type=MESH,
        )

    def gather_copy(e):
        _, device = peer(e)
        return pltpu.make_async_remote_copy(
            src_ref=mine_sum, dst_ref=whole.at[e], send_sem=sems.at[2, e],
            recv_sem=sems.at[3, e], device_id=device, device_id_type=MESH,
        )

    def start(make):
        def body(e, carry):
            make(e).start()
            return carry

        lax.fori_loop(0, n - 1, body, 0)

    def finish(make):
        def body(e, carry):
            make(e).wait()
            return carry

        lax.fori_loop(0, n - 1, body, 0)

    start(scatter_copy)
    lax.fori_loop(0, steps // 2, grad_step, 0)
    finish(scatter_copy)
    total = mine[me].astype(jnp.float32)
    for e in range(n - 1):
        total = total + got[e].astype(jnp.float32)
    mine_sum[...] = total.astype(jnp.bfloat16)
    start(gather_copy)
    out_ref[me] = mine_sum[...].astype(jnp.float32)
    lax.fori_loop(steps // 2, steps, grad_step, 0)
    finish(gather_copy)
    for e in range(n - 1):
        out_ref[lax.rem(me + n - e - 1, n)] = whole[e].astype(jnp.float32)


def per_device(features, depth_kernel, in_weight, out_weight, decoder_weight, observed, land_mask):
    _, channels, lon_len, lat_len = features.shape
    outputs = decoder_weight.shape[1]
    size = depth_kernel.shape[1]
    half = size // 2
    member_n = lax.axis_size("member")
    space_n = lax.axis_size("space")
    n = member_n * space_n
    members = features.shape[0] * member_n
    total_points = lon_len * space_n * lat_len
    padded_c = round_up(channels, 16)

    x = jnp.transpose(features[0], (1, 0, 2))
    forth = [(i, (i + 1) % space_n) for i in range(space_n)]
    back = [((i + 1) % space_n, i) for i in range(space_n)]
    left = lax.ppermute(x[lon_len - half :], "space", forth)
    right = lax.ppermute(x[:half], "space", back)
    taps = jnp.pad(depth_kernel.reshape(channels, size * size), ((0, padded_c - channels), (0, 0)))
    taps = jnp.concatenate([taps, taps, taps], axis=1)
    inner = conv_norm("inner", half, (0,), (x,), taps)
    edge = conv_norm(
        "edge", half, (0, 0, 1, 1), (left, x[: 2 * half], x[lon_len - 2 * half :], right), taps
    )
    weight = 4.0 + 8.0 * land_mask.astype(jnp.float32)
    wide_c = round_up(channels, 128)
    tiles = (outputs // 8) * (wide_c // 128)
    per = -(-tiles // n)
    rows_at_once = half
    grad, summed = pl.pallas_call(
        functools.partial(
            main_kernel, (member_n, space_n), rows_at_once, 1.0 / math.sqrt(members * total_points)
        ),
        name="main",
        out_shape=(
            jax.ShapeDtypeStruct((lon_len, channels, lat_len), jnp.bfloat16),
            jax.ShapeDtypeStruct((n, per * 8, 128), jnp.float32),
        ),
        in_specs=[VMEM_SPEC] * 9,
        out_specs=[VMEM_SPEC] * 2,
        scratch_shapes=[
            pltpu.VMEM((lon_len, channels, lat_len), jnp.bfloat16),
            pltpu.VMEM((lon_len, outputs, lat_len), jnp.bfloat16),
            pltpu.VMEM((member_n - 1, lon_len, outputs, lat_len), jnp.bfloat16),
            pltpu.VMEM((lon_len, outputs, lat_len), jnp.bfloat16),
            pltpu.VMEM((outputs, wide_c), jnp.float32),
            pltpu.VMEM((channels, outputs), jnp.float32),
            pltpu.VMEM((n, per * 8, 128), jnp.bfloat16),
            pltpu.VMEM((n - 1, per * 8, 128), jnp.bfloat16),
            pltpu.VMEM((per * 8, 128), jnp.bfloat16),
            pltpu.VMEM((n - 1, per * 8, 128), jnp.bfloat16),
            pltpu.SemaphoreType.DMA((2, member_n - 1, lon_len // rows_at_once)),
            pltpu.SemaphoreType.DMA((4, n - 1)),
        ],
        compiler_params=pltpu.CompilerParams(collective_id=0, has_side_effects=True),
    )(
        x, inner, edge, in_weight.T, out_weight.T, decoder_weight.T, decoder_weight,
        jnp.transpose(observed, (1, 0, 2)), weight,
    )
    flat = summed.reshape(n * per, 8, 128)[:tiles].reshape(outputs // 8, wide_c // 128, 8, 128)
    decoder_grad = jnp.transpose(flat, (0, 2, 1, 3)).reshape(outputs, wide_c)[:, :channels].T
    grad_features = jnp.transpose(grad, (1, 0, 2))[None]
    return (grad_features, decoder_grad)


def solution(mesh):
    placed = (
        P("member", None, "space", None),
        P(),
        P(),
        P(),
        P(),
        P(None, "space", None),
        P("space", None),
    )
    return jax.shard_map(
        per_device,
        mesh=mesh,
        in_specs=placed,
        out_specs=(P("member", None, "space", None), P()),
        check_vma=False,
    )
```
